512 devices in a mesh: row: 16 (over x, z_hi), col: 32 (over z_lo, y, core).
Axes of the slice: x: 4, y: 4, z: 16 (z_hi: 4, z_lo: 4; z = z_hi * 4 + z_lo), core: 2. Of those that a mesh axis runs over, the one named last changes fastest.
Arguments:
- i_list: int32 [2], replicated, may hold values from 0 to 127
- pairs: int32 [2, 2], replicated, may hold values from 0 to 127
- vir_offsets: int32 [2], replicated, may hold values from 0 to 960, as said below
- occ_energy: float32 [128], replicated, may hold values from -2 to -0.5
- vir_energy: float32 [1024], replicated, may hold values from 0.5 to 5
- amplitudes: bfloat16 [2, 1024, 1024], P(None, 'row', 'col'), may hold values from -6 to 6
- integrals: bfloat16 [2, 1024, 64, 128], P(None, 'row', 'col'), may hold values from -1.75 to 1.75
Outputs:
- density: bfloat16 [2, 1024, 64, 128], P(None, 'row', 'col')
- amp_grad: bfloat16 [2, 1024, 1024], P(None, 'row', 'col')
The draws below stay inside these ranges and needn't reach their ends.
Inputs may be any that keep to these rules, and one draw needn't show every extreme that they name: `vir_offsets`: the first entry is a multiple of 128 and at most 896; the second is at most 960.
All inputs are finite; a program needn't handle non-finite values.
Results may differ from the reference program's by a relative error of at most 0.012.
Values may be sent and summed in bfloat16 or wider, within the bound.
A program may use at most 64 MiB of HBM per device.

```python
import jax
import jax.numpy as jnp
from jax import lax

NOCC = 128
V = 1024
NA = 128
NI = 2
NPAIR = 2
NB = 64


def draw_vir_offsets(key, part):
    key_a = jax.random.fold_in(key, 11)
    key_b = jax.random.fold_in(key, 23)
    if NA <= NB:
        start_a = jnp.full((1,), V - NA, jnp.int32)
        start_b = jax.random.randint(key_b, (1,), 0, V - NB + 1)
    else:
        start_a = jax.random.randint(key_a, (1,), 0, V // NA) * NA
        start_b = jnp.full((1,), V - NB, jnp.int32)
    return jnp.concatenate([start_a.astype(jnp.int32), start_b.astype(jnp.int32)]).astype(jnp.int32)


def with_ends(entries, stream_key, least, top_value):
    longest = entries.shape.index(max(entries.shape))
    spots = []
    for shift in (0, 1):
        where = [jax.random.randint(jax.random.fold_in(stream_key, axis), (), 0, length) for axis, length in enumerate(entries.shape)]
        where[longest] = (where[longest] + shift) % entries.shape[longest]
        spots.append(tuple(where))
    return entries.at[spots[0]].set(least).at[spots[1]].set(top_value)


def strengthened(entries, rng, source, target, blocks, factor):
    owner, partner = [(jnp.arange(entries.shape[axis_at]) // (entries.shape[axis_at] // blocks)).reshape([-1 if axis == axis_at else 1 for axis in range(entries.ndim)]) for axis_at in (source, target)]
    chosen = jax.random.permutation(rng, blocks)[partner]
    strong = (owner == chosen) | (owner == (partner + blocks // 2) % blocks)
    return jnp.where(strong, factor * entries, entries)


def steps_of(own_key, shape, cuts, least, high):
    loudness = 1.0
    for position, parts in cuts:
        heights = jax.random.uniform(jax.random.fold_in(jax.random.fold_in(own_key, 6), position), (parts,), jnp.float32, least / len(cuts), high / len(cuts))
        loudness = loudness * jnp.repeat(jnp.exp(heights), shape[position] // parts).reshape((-1,) + (1,) * (len(shape) - 1 - position))
    return loudness


def noise_with(rng, extent, scale, reach, shards, heavy, kind=jnp.bfloat16):
    drawn = scale * jax.random.normal(rng, extent, jnp.float32)
    if shards:
        drawn = drawn * steps_of(rng, extent, shards, -0.22, 0.18)
    return jnp.clip(strengthened(drawn, jax.random.fold_in(rng, 3), *heavy), -reach, reach).astype(kind)


def setup_inputs(seed: int = 0) -> dict:
    streams_of = jax.random.split(jax.random.key(seed), 8)
    return {
        "i_list": jax.random.randint(streams_of[0], (NI,), 0, NOCC).astype(jnp.int32),
        "pairs": with_ends(jax.random.randint(streams_of[1], (NPAIR, 2), 0, NOCC), jax.random.fold_in(streams_of[1], 1), 0, NOCC - 1).astype(jnp.int32),
        "vir_offsets": draw_vir_offsets(jax.random.fold_in(streams_of[7], 71), 0),
        "occ_energy": jnp.clip(jax.random.uniform(streams_of[3], (NOCC,), jnp.float32, -2.0, -0.5), -2.0, -0.5),
        "vir_energy": jnp.clip(jax.random.uniform(streams_of[4], (V,), jnp.float32, 0.5, 5.0), 0.5, 5.0),
        "amplitudes": noise_with(streams_of[5], (NPAIR, V, V), 0.2, 6.0, ((1, 16), (2, 32)), (1, 2, 32, 2.75)),
        "integrals": noise_with(streams_of[6], (NI, V, NB, NA), 0.06, 1.75, ((1, 16), (2, 32)), (2, 1, 32, 2.75)),
    }


def reference(i_list, pairs, vir_offsets, occ_energy, vir_energy, amplitudes, integrals):
    e_a = lax.dynamic_slice(vir_energy, (vir_offsets[0].astype(jnp.int32),), (NA,))
    e_b = lax.dynamic_slice(vir_energy, (vir_offsets[1].astype(jnp.int32),), (NB,))
    occ_sum = occ_energy[i_list][:, None] + occ_energy[pairs[:, 0]][None, :] + occ_energy[pairs[:, 1]][None, :]
    base = -(vir_energy[:, None, None] + e_b[None, :, None] + e_a[None, None, :]).reshape(V, NB * NA)
    densities = []
    grad_total = jnp.zeros((NPAIR, V, V), jnp.float32)
    for ii in range(NI):
        ints = integrals[ii].reshape(V, NB * NA)
        total = jnp.zeros((V, NB * NA), jnp.float32)
        grads = []
        for pp in range(NPAIR):
            triples = jnp.dot(amplitudes[pp], ints, preferred_element_type=jnp.float32)
            scaled = (triples / (occ_sum[ii, pp] + base)).astype(jnp.bfloat16)
            total = total + lax.dot_general(amplitudes[pp], scaled, (((0,), (0,)), ((), ())), preferred_element_type=jnp.float32)
            grads.append(lax.dot_general(scaled, ints, (((1,), (1,)), ((), ())), preferred_element_type=jnp.float32))
        grad_total = grad_total + jnp.stack(grads)
        densities.append(total.astype(jnp.bfloat16).reshape(V, NB, NA))
    density = jnp.stack(densities)
    return density, grad_total.astype(jnp.bfloat16)
```

```python
import jax
import jax.numpy as jnp
from jax import lax
from jax.experimental import pallas as pl
from jax.experimental.pallas import tpu as pltpu
from jax.sharding import PartitionSpec as P

BF16 = jnp.bfloat16
F32 = jnp.float32
MESH = pl.DeviceIdType.MESH


def pick_energy(index_values, energies):
    table = jnp.arange(energies.shape[0], dtype=jnp.int32)
    onehot = (index_values[..., None] == table).astype(jnp.float32)
    return jnp.sum(onehot * energies, axis=-1)


def kernel(
    amp_in, int_in, row_ref, ea_ref, dens_out, grad_out,
    amp, ints, scaled, grad, grad_core, grad_y, grad_yrecv, grad_z, grad_zrecv,
    dens, dens_xrecv, dens_sum, dens_zrecv,
    az_s, az_r, ay_s, ay_r, ac_s, ac_r, iz_s, iz_r, ix_s, ix_r,
    dx_s, dx_r, dz_s, dz_r, gc_s, gc_r, gy_s, gy_r, gz_s, gz_r,
):
    row = lax.axis_index("row")
    col = lax.axis_index("col")
    x, zh = row // 4, row % 4
    zl, y, core = col // 8, (col // 2) % 4, col % 2
    z = zh * 4 + zl

    def z_peer(o):
        t = (z + o) % 16
        return (x * 4 + t // 4, (t % 4) * 8 + y * 2 + core)

    def zh_peer(k):
        return (x * 4 + (zh + k) % 4, col)

    def x_peer(j):
        return (((x + j) % 4) * 4 + zh, col)

    def y_peer(j):
        return (row, zl * 8 + ((y + j) % 4) * 2 + core)

    core_peer = (row, col + 1 - 2 * core)

    def remote(src, dst, ssem, rsem, dev):
        return pltpu.make_async_remote_copy(
            src_ref=src, dst_ref=dst, send_sem=ssem, recv_sem=rsem,
            device_id=dev, device_id_type=MESH,
        )

    barrier = pltpu.get_barrier_semaphore()

    def greet(dev):
        pl.semaphore_signal(barrier, inc=1, device_id=dev, device_id_type=MESH)

    @pl.loop(1, 16)
    def _(o):
        greet(z_peer(o))

    for j in range(1, 4):
        greet(x_peer(j))
        greet(y_peer(j))
    greet(core_peer)
    pl.semaphore_wait(barrier, 22)

    def amp_z(o):
        return remote(amp_in, amp.at[zh, zl, y, core], az_s.at[o], az_r.at[o], z_peer(o))

    @pl.loop(1, 16)
    def _(k):
        o = (8 + ((k + 0) // 2) * (2 * (k % 2) - 1) + 16) % 16
        amp_z(o).start()

    def int_z(k):
        return remote(int_in.at[(zh + k) % 4], ints.at[row], iz_s.at[k], iz_r.at[k], zh_peer(k))

    for k in (2, 1, 3):
        int_z(k).start()

    amp[zh, zl, y, core] = amp_in[...]
    ints[row] = int_in[zh]

    def amp_piece(o):
        s = (z - o + 16) % 16
        return s // 4, s % 4

    def amp_y(o, j):
        h, l = amp_piece(o)
        block = amp.at[h, l, y, core]
        return remote(block, block, ay_s.at[o, j], ay_r.at[o, j], y_peer(j))

    def amp_y_own(j):
        return remote(amp_in, amp.at[zh, zl, y, core], ay_s.at[0, j], ay_r.at[0, j], y_peer(j))

    def amp_c(o):
        h, l = amp_piece(o)
        block = amp.at[h, l, :, core]
        return remote(block, block, ac_s.at[o], ac_r.at[o], core_peer)

    def int_x(k, j):
        block = ints.at[x * 4 + (zh - k + 4) % 4]
        src = int_in.at[zh] if k == 0 else block
        return remote(src, block, ix_s.at[k, j], ix_r.at[k, j], x_peer(j))

    for j in (2, 1, 3):
        amp_y_own(j).start()
        int_x(0, j).start()

    @pl.loop(1, 16)
    def _(k):
        o = ((k // 2) * (1 - 2 * (k % 2)) - (k % 2) + 16) % 16
        amp_z(o).wait_recv()
        for j in (2, 1, 3):
            amp_y(o, j).start()

    for k in (1, 3, 2):
        int_z(k).wait_recv()
        for j in (2, 1, 3):
            int_x(k, j).start()

    for j in (1, 2, 3):
        amp_y_own(j).wait_recv()
    amp_c(0).start()

    @pl.loop(1, 16)
    def _(k):
        o = ((k // 2) * (1 - 2 * (k % 2)) - (k % 2) + 16) % 16
        for j in (1, 2, 3):
            amp_y(o, j).wait_recv()
        amp_c(o).start()

    for k in (0, 1, 3, 2):
        for j in (1, 2, 3):
            int_x(k, j).wait_recv()
    ints_all = ints[...].reshape(1024, 128)
    ints_t = ints_all.T

    @pl.loop(0, 16)
    def _(o):
        amp_c(o).wait_recv()

    for h in range(4):
        t = jnp.dot(ints_t, amp[h].reshape(1024, 128), preferred_element_type=F32)
        scaled[h] = (t / (row_ref[h] - ea_ref[...])).astype(BF16)

    def grad_c(h):
        return remote(
            grad.at[h, :, :, 1 - core], grad_core.at[h], gc_s.at[h], gc_r.at[h], core_peer
        )

    for k in (2, 1, 3, 0):
        h = (zh + k) % 4
        g = jnp.dot(ints_all, scaled[h], preferred_element_type=F32)
        grad[h] = g.astype(BF16).reshape(4, 4, 2, 32, 128)
        grad_c(h).start()

    def dens_x(j):
        return remote(
            dens.at[(x + j) % 4], dens_xrecv.at[j], dx_s.at[j], dx_r.at[j], x_peer(j)
        )

    for j in (2, 1, 3, 0):
        t = (x + j) % 4
        acc = jnp.zeros((256, 128), F32)
        for h in range(4):
            acc += lax.dot_general(
                amp[h, t].reshape(256, 128), scaled[h], (((1,), (1,)), ((), ())),
                preferred_element_type=F32,
            )
        dens[t] = acc.astype(BF16).reshape(4, 64, 128)
        if j:
            dens_x(j).start()

    def grad_yc(k, j):
        h = (zh + k) % 4
        return remote(
            grad_y.at[h, :, (y + j) % 4], grad_yrecv.at[k, j], gy_s.at[k, j], gy_r.at[k, j],
            y_peer(j),
        )

    for k in (2, 1, 3, 0):
        h = (zh + k) % 4
        grad_c(h).wait_recv()
        s = grad[h, :, :, core].astype(F32) + grad_core[h].astype(F32)
        grad_y[h] = s.astype(BF16)
        for j in (2, 1, 3):
            grad_yc(k, j).start()

    def dens_z(k):
        return remote(
            dens_sum.at[(zh + k) % 4], dens_zrecv.at[k], dz_s.at[k], dz_r.at[k], zh_peer(k)
        )

    total = dens[x].astype(F32)
    for j in (1, 3, 2):
        dens_x(j).wait_recv()
        total += dens_xrecv[j].astype(F32)
    dens_sum[...] = total.astype(BF16)
    for k in (2, 1, 3):
        dens_z(k).start()

    def grad_zc(k, m):
        t = (zl + m) % 4
        o = (4 * k + t - zl + 16) % 16
        return remote(
            grad_z.at[(zh + k) % 4, t], grad_zrecv.at[o], gz_s.at[o], gz_r.at[o], z_peer(o)
        )

    for k in (2, 1, 3, 0):
        h = (zh + k) % 4
        s = grad_y[h, :, y].astype(F32)
        for j in (1, 3, 2):
            grad_yc(k, j).wait_recv()
            s += grad_yrecv[k, j].astype(F32)
        grad_z[h] = s.astype(BF16)
        for m in range(4):
            if k or m:
                grad_zc(k, m).start()

    dens_out[zh] = dens_sum[zh]
    for k in (1, 3, 2):
        dens_z(k).wait_recv()
        dens_out[(zh - k + 4) % 4] = dens_zrecv[k]

    def grad_zo(o):
        return remote(
            grad_z.at[0, 0], grad_zrecv.at[o], gz_s.at[o], gz_r.at[o], z_peer(o)
        )

    def add_z(o, s):
        grad_zo(o).wait_recv()
        return s + grad_zrecv[o].astype(F32)

    s = lax.fori_loop(1, 16, add_z, grad_z[zh, zl].astype(F32))
    grad_out[...] = s.T.astype(BF16)

    @pl.loop(1, 16)
    def _(o):
        amp_z(o).wait_send()
        grad_zo(o).wait_send()

    @pl.loop(0, 16)
    def _(o):
        for j in (1, 2, 3):
            amp_y(o, j).wait_send()
        amp_c(o).wait_send()

    for k in range(4):
        for j in (1, 2, 3):
            int_x(k, j).wait_send()
            grad_yc(k, j).wait_send()
        grad_c(k).wait_send()
    for k in (1, 2, 3):
        int_z(k).wait_send()
        dens_x(k).wait_send()
        dens_z(k).wait_send()


def local(i_list, pairs, vir_offsets, occ_energy, vir_energy, amplitudes, integrals):
    row = lax.axis_index("row")
    col = lax.axis_index("col")
    x, zh = row // 4, row % 4
    occ = (
        pick_energy(i_list, occ_energy)[:, None]
        + pick_energy(pairs[:, 0], occ_energy)[None, :]
        + pick_energy(pairs[:, 1], occ_energy)[None, :]
    )
    occ = jnp.where(zh // 2 == 0, occ[0], occ[1])
    e_c = lax.dynamic_slice_in_dim(vir_energy, x * 256, 256).reshape(4, 1, 64)
    e_b = lax.dynamic_slice_in_dim(vir_energy, vir_offsets[1] + col * 2 + zh % 2, 1)
    e_a = lax.dynamic_slice_in_dim(vir_energy, vir_offsets[0], 128)
    row_part = (occ[None, :, None] - (e_c + e_b[0])).reshape(4, 1, 128)
    e_a = jnp.broadcast_to(e_a[:, None], (128, 128))
    amp_t = amplitudes.transpose(2, 0, 1).reshape(32, 128)
    ints_t = integrals.transpose(0, 2, 1, 3).reshape(4, 64, 128)
    vmem = pl.BlockSpec(memory_space=pltpu.VMEM)
    dma = pltpu.SemaphoreType.DMA
    dens, grad = pl.pallas_call(
        kernel,
        out_shape=(
            jax.ShapeDtypeStruct((4, 64, 128), BF16),
            jax.ShapeDtypeStruct((128, 32), BF16),
        ),
        in_specs=[vmem] * 4,
        out_specs=(vmem, vmem),
        scratch_shapes=[
            pltpu.VMEM((4, 4, 4, 2, 32, 128), BF16),
            pltpu.VMEM((16, 64, 128), BF16),
            pltpu.VMEM((4, 128, 128), BF16),
            pltpu.VMEM((4, 4, 4, 2, 32, 128), BF16),
            pltpu.VMEM((4, 4, 4, 32, 128), BF16),
            pltpu.VMEM((4, 4, 4, 32, 128), BF16),
            pltpu.VMEM((4, 4, 4, 32, 128), BF16),
            pltpu.VMEM((4, 4, 32, 128), BF16),
            pltpu.VMEM((16, 32, 128), BF16),
            pltpu.VMEM((4, 4, 64, 128), BF16),
            pltpu.VMEM((4, 4, 64, 128), BF16),
            pltpu.VMEM((4, 64, 128), BF16),
            pltpu.VMEM((4, 64, 128), BF16),
            dma((16,)), dma((16,)), dma((16, 4)), dma((16, 4)), dma((16,)), dma((16,)),
            dma((4,)), dma((4,)), dma((4, 4)), dma((4, 4)),
            dma((4,)), dma((4,)), dma((4,)), dma((4,)),
            dma((4,)), dma((4,)), dma((4, 4)), dma((4, 4)), dma((16,)), dma((16,)),
        ],
        compiler_params=pltpu.CompilerParams(collective_id=0, has_side_effects=True),
    )(amp_t, ints_t, row_part, e_a)
    density = dens.reshape(2, 2, 64, 128).transpose(0, 2, 1, 3)
    return density, grad.reshape(2, 64, 32)


def solution(mesh):
    return jax.shard_map(
        local,
        mesh=mesh,
        in_specs=(P(), P(), P(), P(), P(), P(None, "row", "col"), P(None, "row", "col", None)),
        out_specs=(P(None, "row", "col", None), P(None, "row", "col")),
        check_vma=False,
    )
```

```python
import jax
import jax.numpy as jnp
from jax import lax
from jax.experimental import pallas as pl
from jax.experimental.pallas import tpu as pltpu
from jax.sharding import PartitionSpec as P

BF16 = jnp.bfloat16
F32 = jnp.float32
MESH = pl.DeviceIdType.MESH


def kernel(
    i_list, pairs, vir_offsets, occ_energy, vir_energy, vir_rows, amp_hbm, int_hbm,
    dens_out, grad_out,
    i_sm, pairs_sm, off_sm, occ_sm, vir_sm, vir_vm, amp_vm, int_vm, amp_in, int_in, in_sem,
    amp, ints, scaled, grad, grad_core, grad_y, grad_yrecv, grad_z, grad_zrecv,
    dens, dens_xrecv, dens_sum, dens_zrecv,
    az_s, az_r, ay_s, ay_r, ac_s, ac_r, iz_s, iz_r, ix_s, ix_r,
    dx_s, dx_r, dz_s, dz_r, gc_s, gc_r, gy_s, gy_r, gz_s, gz_r,
):
    row = lax.axis_index("row")
    col = lax.axis_index("col")
    x, zh = row // 4, row % 4
    zl, y, core = col // 8, (col // 2) % 4, col % 2
    z = zh * 4 + zl

    def z_peer(o):
        t = (z + o) % 16
        return (x * 4 + t // 4, (t % 4) * 8 + y * 2 + core)

    def zh_peer(k):
        return (x * 4 + (zh + k) % 4, col)

    def x_peer(j):
        return (((x + j) % 4) * 4 + zh, col)

    def y_peer(j):
        return (row, zl * 8 + ((y + j) % 4) * 2 + core)

    core_peer = (row, col + 1 - 2 * core)

    def remote(src, dst, ssem, rsem, dev):
        return pltpu.make_async_remote_copy(
            src_ref=src, dst_ref=dst, send_sem=ssem, recv_sem=rsem,
            device_id=dev, device_id_type=MESH,
        )

    loads = [
        pltpu.make_async_copy(src, dst, in_sem.at[n])
        for n, (src, dst) in enumerate((
            (amp_hbm, amp_vm), (int_hbm, int_vm), (vir_rows, vir_vm), (i_list, i_sm),
            (pairs, pairs_sm), (vir_offsets, off_sm), (occ_energy, occ_sm), (vir_energy, vir_sm),
        ))
    ]
    for load in loads:
        load.start()

    barrier = pltpu.get_barrier_semaphore()

    def greet(dev):
        pl.semaphore_signal(barrier, inc=1, device_id=dev, device_id_type=MESH)

    @pl.loop(1, 16)
    def _(o):
        greet(z_peer(o))

    for j in range(1, 4):
        greet(x_peer(j))
        greet(y_peer(j))
    greet(core_peer)
    loads[0].wait()
    amp_in[...] = jnp.concatenate([amp_vm[0], amp_vm[1]], axis=1)
    amp[zh, zl, y, core] = amp_in[...]
    pl.semaphore_wait(barrier, 22)

    def amp_z(o):
        return remote(amp_in, amp.at[zh, zl, y, core], az_s.at[o], az_r.at[o], z_peer(o))

    @pl.loop(1, 16)
    def _(k):
        o = (8 + ((k + 0) // 2) * (2 * (k % 2) - 1) + 16) % 16
        amp_z(o).start()

    loads[1].wait()
    for i in range(2):
        v = int_vm[i].astype(F32)
        for b in range(2):
            int_in[2 * i + b] = v[:, b, :].astype(BF16)

    def int_z(k):
        return remote(int_in.at[(zh + k) % 4], ints.at[row], iz_s.at[k], iz_r.at[k], zh_peer(k))

    for k in (2, 1, 3):
        int_z(k).start()

    ints[row] = int_in[zh]

    def amp_piece(o):
        s = (z - o + 16) % 16
        return s // 4, s % 4

    def amp_y(o, j):
        h, l = amp_piece(o)
        block = amp.at[h, l, y, core]
        return remote(block, block, ay_s.at[o, j], ay_r.at[o, j], y_peer(j))

    def amp_y_own(j):
        return remote(amp_in, amp.at[zh, zl, y, core], ay_s.at[0, j], ay_r.at[0, j], y_peer(j))

    def amp_c(o):
        h, l = amp_piece(o)
        block = amp.at[h, l, :, core]
        return remote(block, block, ac_s.at[o], ac_r.at[o], core_peer)

    def int_x(k, j):
        block = ints.at[x * 4 + (zh - k + 4) % 4]
        src = int_in.at[zh] if k == 0 else block
        return remote(src, block, ix_s.at[k, j], ix_r.at[k, j], x_peer(j))

    for j in (2, 1, 3):
        amp_y_own(j).start()
        int_x(0, j).start()

    for load in loads[2:]:
        load.wait()
    e_a = jnp.broadcast_to(vir_vm[pl.ds(off_sm[0] // 128, 1), :], (128, 128)).T
    e_b = vir_sm[off_sm[1] + col * 2 + zh % 2]
    e_i = occ_sm[i_sm[zh // 2]]
    occ0 = e_i + occ_sm[pairs_sm[0, 0]] + occ_sm[pairs_sm[0, 1]]
    occ1 = e_i + occ_sm[pairs_sm[1, 0]] + occ_sm[pairs_sm[1, 1]]
    first = lax.broadcasted_iota(jnp.int32, (1, 128), 1) < 64
    occ = jnp.where(first, occ0, occ1)
    row_part = []
    for h in range(4):
        e_c = vir_vm[pl.ds(x * 2 + h // 2, 1), :]
        turned = pltpu.roll(e_c, 64, axis=1)
        e_c = jnp.where(first, turned, e_c) if h % 2 else jnp.where(first, e_c, turned)
        row_part.append(occ - (e_c + e_b))

    @pl.loop(1, 16)
    def _(k):
        o = ((k // 2) * (1 - 2 * (k % 2)) - (k % 2) + 16) % 16
        amp_z(o).wait_recv()
        for j in (2, 1, 3):
            amp_y(o, j).start()

    for k in (1, 3, 2):
        int_z(k).wait_recv()
        for j in (2, 1, 3):
            int_x(k, j).start()

    for j in (1, 2, 3):
        amp_y_own(j).wait_recv()
    amp_c(0).start()

    @pl.loop(1, 16)
    def _(k):
        o = ((k // 2) * (1 - 2 * (k % 2)) - (k % 2) + 16) % 16
        for j in (1, 2, 3):
            amp_y(o, j).wait_recv()
        amp_c(o).start()

    for k in (0, 1, 3, 2):
        for j in (1, 2, 3):
            int_x(k, j).wait_recv()
    ints_all = ints[...].reshape(1024, 128)
    ints_t = ints_all.T

    @pl.loop(0, 16)
    def _(o):
        amp_c(o).wait_recv()

    for h in range(4):
        t = jnp.dot(ints_t, amp[h].reshape(1024, 128), preferred_element_type=F32)
        scaled[h] = (t / (row_part[h] - e_a)).astype(BF16)

    def grad_c(h):
        return remote(
            grad.at[h, :, :, 1 - core], grad_core.at[h], gc_s.at[h], gc_r.at[h], core_peer
        )

    for k in (2, 1, 3, 0):
        h = (zh + k) % 4
        g = jnp.dot(ints_all, scaled[h], preferred_element_type=F32)
        grad[h] = g.astype(BF16).reshape(4, 4, 2, 32, 128)
        grad_c(h).start()

    def dens_x(j):
        return remote(
            dens.at[(x + j) % 4], dens_xrecv.at[j], dx_s.at[j], dx_r.at[j], x_peer(j)
        )

    for j in (2, 1, 3, 0):
        t = (x + j) % 4
        acc = jnp.zeros((256, 128), F32)
        for h in range(4):
            acc += lax.dot_general(
                amp[h, t].reshape(256, 128), scaled[h], (((1,), (1,)), ((), ())),
                preferred_element_type=F32,
            )
        dens[t] = acc.astype(BF16).reshape(4, 64, 128)
        if j:
            dens_x(j).start()

    def grad_yc(k, j):
        h = (zh + k) % 4
        return remote(
            grad_y.at[h, :, (y + j) % 4], grad_yrecv.at[k, j], gy_s.at[k, j], gy_r.at[k, j],
            y_peer(j),
        )

    for k in (2, 1, 3, 0):
        h = (zh + k) % 4
        grad_c(h).wait_recv()
        s = grad[h, :, :, core].astype(F32) + grad_core[h].astype(F32)
        grad_y[h] = s.astype(BF16)
        for j in (2, 1, 3):
            grad_yc(k, j).start()

    def dens_z(k):
        return remote(
            dens_sum.at[(zh + k) % 4], dens_zrecv.at[k], dz_s.at[k], dz_r.at[k], zh_peer(k)
        )

    total = dens[x].astype(F32)
    for j in (1, 3, 2):
        dens_x(j).wait_recv()
        total += dens_xrecv[j].astype(F32)
    dens_sum[...] = total.astype(BF16)
    for k in (2, 1, 3):
        dens_z(k).start()

    def grad_zc(k, m):
        t = (zl + m) % 4
        o = (4 * k + t - zl + 16) % 16
        return remote(
            grad_z.at[(zh + k) % 4, t], grad_zrecv.at[o], gz_s.at[o], gz_r.at[o], z_peer(o)
        )

    for k in (2, 1, 3, 0):
        h = (zh + k) % 4
        s = grad_y[h, :, y].astype(F32)
        for j in (1, 3, 2):
            grad_yc(k, j).wait_recv()
            s += grad_yrecv[k, j].astype(F32)
        grad_z[h] = s.astype(BF16)
        for m in range(4):
            if k or m:
                grad_zc(k, m).start()

    dens_out[zh] = dens_sum[zh]
    for k in (1, 3, 2):
        dens_z(k).wait_recv()
        dens_out[(zh - k + 4) % 4] = dens_zrecv[k]

    def grad_zo(o):
        return remote(
            grad_z.at[0, 0], grad_zrecv.at[o], gz_s.at[o], gz_r.at[o], z_peer(o)
        )

    def add_z(o, s):
        grad_zo(o).wait_recv()
        return s + grad_zrecv[o].astype(F32)

    s = lax.fori_loop(1, 16, add_z, grad_z[zh, zl].astype(F32))
    grad_out[0] = s[:, :64].astype(BF16)
    grad_out[1] = s[:, 64:].astype(BF16)

    @pl.loop(1, 16)
    def _(o):
        amp_z(o).wait_send()
        grad_zo(o).wait_send()

    @pl.loop(0, 16)
    def _(o):
        for j in (1, 2, 3):
            amp_y(o, j).wait_send()
        amp_c(o).wait_send()

    for k in range(4):
        for j in (1, 2, 3):
            int_x(k, j).wait_send()
            grad_yc(k, j).wait_send()
        grad_c(k).wait_send()
    for k in (1, 2, 3):
        int_z(k).wait_send()
        dens_x(k).wait_send()
        dens_z(k).wait_send()


def local(i_list, pairs, vir_offsets, occ_energy, vir_energy, amplitudes, integrals):
    hbm = pl.BlockSpec(memory_space=pltpu.HBM)
    vmem = pl.BlockSpec(memory_space=pltpu.VMEM)
    dma = pltpu.SemaphoreType.DMA
    dens, grad = pl.pallas_call(
        kernel,
        out_shape=(
            jax.ShapeDtypeStruct((4, 64, 128), BF16),
            jax.ShapeDtypeStruct((2, 32, 64), BF16),
        ),
        in_specs=[hbm] * 8,
        out_specs=(vmem, vmem),
        scratch_shapes=[
            pltpu.SMEM((2,), jnp.int32), pltpu.SMEM((2, 2), jnp.int32),
            pltpu.SMEM((2,), jnp.int32), pltpu.SMEM((128,), F32), pltpu.SMEM((1024,), F32),
            pltpu.VMEM((8, 128), F32), pltpu.VMEM((2, 32, 64), BF16),
            pltpu.VMEM((2, 64, 2, 128), BF16), pltpu.VMEM((32, 128), BF16),
            pltpu.VMEM((4, 64, 128), BF16), dma((8,)),
            pltpu.VMEM((4, 4, 4, 2, 32, 128), BF16),
            pltpu.VMEM((16, 64, 128), BF16),
            pltpu.VMEM((4, 128, 128), BF16),
            pltpu.VMEM((4, 4, 4, 2, 32, 128), BF16),
            pltpu.VMEM((4, 4, 4, 32, 128), BF16),
            pltpu.VMEM((4, 4, 4, 32, 128), BF16),
            pltpu.VMEM((4, 4, 4, 32, 128), BF16),
            pltpu.VMEM((4, 4, 32, 128), BF16),
            pltpu.VMEM((16, 32, 128), BF16),
            pltpu.VMEM((4, 4, 64, 128), BF16),
            pltpu.VMEM((4, 4, 64, 128), BF16),
            pltpu.VMEM((4, 64, 128), BF16),
            pltpu.VMEM((4, 64, 128), BF16),
            dma((16,)), dma((16,)), dma((16, 4)), dma((16, 4)), dma((16,)), dma((16,)),
            dma((4,)), dma((4,)), dma((4, 4)), dma((4, 4)),
            dma((4,)), dma((4,)), dma((4,)), dma((4,)),
            dma((4,)), dma((4,)), dma((4, 4)), dma((4, 4)), dma((16,)), dma((16,)),
        ],
        compiler_params=pltpu.CompilerParams(collective_id=0, has_side_effects=True),
    )(
        i_list, pairs, vir_offsets, occ_energy, vir_energy, vir_energy.reshape(8, 128),
        amplitudes.transpose(0, 2, 1), integrals,
    )
    density = dens.reshape(2, 2, 64, 128).transpose(0, 2, 1, 3)
    return density, grad.transpose(0, 2, 1)


def solution(mesh):
    return jax.shard_map(
        local,
        mesh=mesh,
        in_specs=(P(), P(), P(), P(), P(), P(None, "row", "col"), P(None, "row", "col", None)),
        out_specs=(P(None, "row", "col", None), P(None, "row", "col")),
        check_vma=False,
    )
```

```python
import jax
import jax.numpy as jnp
from jax import lax
from jax.experimental import pallas as pl
from jax.experimental.pallas import tpu as pltpu
from jax.sharding import PartitionSpec as P

BF16 = jnp.bfloat16
F32 = jnp.float32
MESH = pl.DeviceIdType.MESH


def kernel(
    i_list, pairs, vir_offsets, occ_energy, vir_energy, vir_rows, amp_hbm, int_hbm,
    dens_out, grad_out,
    i_sm, pairs_sm, off_sm, occ_sm, vir_sm, vir_vm, amp_vm, int_vm, amp_in, int_in, in_sem, relay, ir_s, ir_r,
    amp, ints, scaled, grad, grad_core, grad_y, grad_yrecv, grad_z, grad_zrecv,
    dens, dens_xrecv, dens_sum, dens_zrecv,
    az_s, az_r, ay_s, ay_r, ac_s, ac_r, iz_s, iz_r, ix_s, ix_r,
    dx_s, dx_r, dz_s, dz_r, gc_s, gc_r, gy_s, gy_r, gz_s, gz_r,
):
    row = lax.axis_index("row")
    col = lax.axis_index("col")
    x, zh = row // 4, row % 4
    zl, y, core = col // 8, (col // 2) % 4, col % 2
    z = zh * 4 + zl

    def z_peer(o):
        t = (z + o) % 16
        return (x * 4 + t // 4, (t % 4) * 8 + y * 2 + core)

    def zh_peer(k):
        return (x * 4 + (zh + k) % 4, col)

    def x_peer(j):
        return (((x + j) % 4) * 4 + zh, col)

    def y_peer(j):
        return (row, zl * 8 + ((y + j) % 4) * 2 + core)

    core_peer = (row, col + 1 - 2 * core)

    def remote(src, dst, ssem, rsem, dev):
        return pltpu.make_async_remote_copy(
            src_ref=src, dst_ref=dst, send_sem=ssem, recv_sem=rsem,
            device_id=dev, device_id_type=MESH,
        )

    loads = [
        pltpu.make_async_copy(src, dst, in_sem.at[n])
        for n, (src, dst) in enumerate((
            (amp_hbm, amp_vm), (int_hbm, int_vm), (vir_rows, vir_vm), (i_list, i_sm),
            (pairs, pairs_sm), (vir_offsets, off_sm), (occ_energy, occ_sm), (vir_energy, vir_sm),
        ))
    ]
    for load in loads:
        load.start()

    barrier = pltpu.get_barrier_semaphore()

    def greet(dev):
        pl.semaphore_signal(barrier, inc=1, device_id=dev, device_id_type=MESH)

    for o in (1, 2, 3, 4, 12, 13, 14, 15):
        greet(z_peer(o))
    for j in range(1, 4):
        greet(x_peer(j))
        greet(y_peer(j))
    greet(core_peer)
    loads[0].wait()
    amp_in[...] = jnp.concatenate([amp_vm[0], amp_vm[1]], axis=1)
    amp[zh, zl, y, core] = amp_in[...]
    pl.semaphore_wait(barrier, 15)

    def amp_z(o):
        return remote(amp_in, amp.at[zh, zl, y, core], az_s.at[o], az_r.at[o], z_peer(o))

    for o in (4, 12, 3, 13, 2, 14, 1, 15):
        amp_z(o).start()

    loads[1].wait()
    for i in range(2):
        v = int_vm[i].astype(F32)
        for b in range(2):
            int_in[2 * i + b] = v[:, b, :].astype(BF16)

    def int_z(k):
        return remote(int_in.at[(zh + k) % 4], ints.at[row], iz_s.at[k], iz_r.at[k], zh_peer(k))

    def int_relay(n):
        return remote(
            int_in.at[(zh + 2) % 4, pl.ds(32 * n, 32)], relay.at[n], ir_s.at[n], ir_r.at[n],
            zh_peer(1 + 2 * n),
        )

    def int_onward(n):
        k = 1 + 2 * n
        return remote(
            relay.at[n], ints.at[x * 4 + (zh + 4 - k) % 4, pl.ds(32 * n, 32)],
            iz_s.at[2 - 2 * n], iz_r.at[2 - 2 * n], zh_peer(k),
        )

    for n in range(2):
        int_relay(n).start()
    for k in (1, 3):
        int_z(k).start()

    ints[row] = int_in[zh]

    def amp_piece(o):
        s = (z - o + 16) % 16
        return s // 4, s % 4

    def amp_y(o, j):
        h, l = amp_piece(o)
        block = amp.at[h, l, y, core]
        return remote(block, block, ay_s.at[o, j], ay_r.at[o, j], y_peer(j))

    def amp_y_own(j):
        return remote(amp_in, amp.at[zh, zl, y, core], ay_s.at[0, j], ay_r.at[0, j], y_peer(j))

    def amp_c(o):
        h, l = amp_piece(o)
        block = amp.at[h, l, :, core]
        return remote(block, block, ac_s.at[o], ac_r.at[o], core_peer)

    def int_x(k, j):
        block = ints.at[x * 4 + (zh - k + 4) % 4]
        src = int_in.at[zh] if k == 0 else block
        return remote(src, block, ix_s.at[k, j], ix_r.at[k, j], x_peer(j))

    for j in (2, 1, 3):
        amp_y_own(j).start()
        int_x(0, j).start()

    for load in loads[2:]:
        load.wait()
    e_a = jnp.broadcast_to(vir_vm[pl.ds(off_sm[0] // 128, 1), :], (128, 128)).T
    e_b = vir_sm[off_sm[1] + col * 2 + zh % 2]
    e_i = occ_sm[i_sm[zh // 2]]
    occ0 = e_i + occ_sm[pairs_sm[0, 0]] + occ_sm[pairs_sm[0, 1]]
    occ1 = e_i + occ_sm[pairs_sm[1, 0]] + occ_sm[pairs_sm[1, 1]]
    first = lax.broadcasted_iota(jnp.int32, (1, 128), 1) < 64
    occ = jnp.where(first, occ0, occ1)
    row_part = []
    for h in range(4):
        e_c = vir_vm[pl.ds(x * 2 + h // 2, 1), :]
        turned = pltpu.roll(e_c, 64, axis=1)
        e_c = jnp.where(first, turned, e_c) if h % 2 else jnp.where(first, e_c, turned)
        row_part.append(occ - (e_c + e_b))

    def amp_on(o):
        near = 4 if o < 8 else 12
        h, l = amp_piece(near)
        block = amp.at[h, l, y, core]
        return remote(block, block, az_s.at[o], az_r.at[o], z_peer((o - near) % 16))

    def amp_half(n):
        near = 4 if n == 0 else 12
        h, l = amp_piece(near)
        block = amp.at[h, l, y, core, pl.ds(16 * n, 16)]
        return remote(block, block, az_s.at[8 - 8 * n], az_r.at[8 - 8 * n], z_peer(near))

    for o in (1, 15, 2, 14, 4, 12, 3, 13, 5, 11, 6, 10, 7, 9, 8):
        if o == 8:
            amp_half(0).wait_recv()
            amp_half(1).wait_recv()
        else:
            amp_z(o).wait_recv()
        if o == 4:
            amp_half(0).start()
            for t in (7, 6, 5):
                amp_on(t).start()
        if o == 12:
            amp_half(1).start()
            for t in (9, 10, 11):
                amp_on(t).start()
        for j in (2, 1, 3):
            amp_y(o, j).start()
        if o == 13:
            for n in range(2):
                int_relay(n).wait_recv()
                int_onward(n).start()
            for k in (1, 3):
                int_z(k).wait_recv()
                for j in (2, 1, 3):
                    int_x(k, j).start()

    for n in range(2):
        int_onward(n).wait_recv()
    for j in (2, 1, 3):
        int_x(2, j).start()

    for j in (1, 2, 3):
        amp_y_own(j).wait_recv()
    amp_c(0).start()

    for o in (1, 15, 2, 14, 4, 12, 3, 13, 5, 11, 6, 10, 7, 9, 8):
        for j in (1, 2, 3):
            amp_y(o, j).wait_recv()
        amp_c(o).start()

    for k in (0, 1, 3, 2):
        for j in (1, 2, 3):
            int_x(k, j).wait_recv()
    ints_all = ints[...].reshape(1024, 128)
    ints_t = ints_all.T

    @pl.loop(0, 16)
    def _(o):
        amp_c(o).wait_recv()

    for h in range(4):
        t = jnp.dot(ints_t, amp[h].reshape(1024, 128), preferred_element_type=F32)
        scaled[h] = (t / (row_part[h] - e_a)).astype(BF16)

    def grad_c(h):
        return remote(
            grad.at[h, :, :, 1 - core], grad_core.at[h], gc_s.at[h], gc_r.at[h], core_peer
        )

    for k in (2, 1, 3, 0):
        h = (zh + k) % 4
        g = jnp.dot(ints_all, scaled[h], preferred_element_type=F32)
        grad[h] = g.astype(BF16).reshape(4, 4, 2, 32, 128)
        grad_c(h).start()

    def dens_x(j):
        return remote(
            dens.at[(x + j) % 4], dens_xrecv.at[j], dx_s.at[j], dx_r.at[j], x_peer(j)
        )

    for j in (2, 1, 3, 0):
        t = (x + j) % 4
        acc = jnp.zeros((256, 128), F32)
        for h in range(4):
            acc += lax.dot_general(
                amp[h, t].reshape(256, 128), scaled[h], (((1,), (1,)), ((), ())),
                preferred_element_type=F32,
            )
        dens[t] = acc.astype(BF16).reshape(4, 64, 128)
        if j:
            dens_x(j).start()

    def grad_yc(k, j):
        h = (zh + k) % 4
        return remote(
            grad_y.at[h, :, (y + j) % 4], grad_yrecv.at[k, j], gy_s.at[k, j], gy_r.at[k, j],
            y_peer(j),
        )

    for k in (2, 1, 3, 0):
        h = (zh + k) % 4
        grad_c(h).wait_recv()
        s = grad[h, :, :, core].astype(F32) + grad_core[h].astype(F32)
        grad_y[h] = s.astype(BF16)
        for j in (2, 1, 3):
            grad_yc(k, j).start()

    def dens_z(k):
        return remote(
            dens_sum.at[(zh + k) % 4], dens_zrecv.at[k], dz_s.at[k], dz_r.at[k], zh_peer(k)
        )

    total = dens[x].astype(F32)
    for j in (1, 3, 2):
        dens_x(j).wait_recv()
        total += dens_xrecv[j].astype(F32)
    dens_sum[...] = total.astype(BF16)
    for k in (2, 1, 3):
        dens_z(k).start()

    def grad_zc(k, m):
        t = (zl + m) % 4
        o = (4 * k + t - zl + 16) % 16
        return remote(
            grad_z.at[(zh + k) % 4, t], grad_zrecv.at[o], gz_s.at[o], gz_r.at[o], z_peer(o)
        )

    for k in (2, 1, 3, 0):
        h = (zh + k) % 4
        s = grad_y[h, :, y].astype(F32)
        for j in (1, 3, 2):
            grad_yc(k, j).wait_recv()
            s += grad_yrecv[k, j].astype(F32)
        grad_z[h] = s.astype(BF16)
        for m in range(4):
            if k or m:
                grad_zc(k, m).start()

    dens_out[zh] = dens_sum[zh]
    for k in (1, 3, 2):
        dens_z(k).wait_recv()
        dens_out[(zh - k + 4) % 4] = dens_zrecv[k]

    def grad_zo(o):
        return remote(
            grad_z.at[0, 0], grad_zrecv.at[o], gz_s.at[o], gz_r.at[o], z_peer(o)
        )

    def add_z(o, s):
        grad_zo(o).wait_recv()
        return s + grad_zrecv[o].astype(F32)

    s = lax.fori_loop(1, 16, add_z, grad_z[zh, zl].astype(F32))
    grad_out[0] = s[:, :64].astype(BF16)
    grad_out[1] = s[:, 64:].astype(BF16)

    for o in (1, 2, 3, 4, 5, 6, 7, 9, 10, 11, 12, 13, 14, 15):
        amp_z(o).wait_send()
    for n in range(2):
        amp_half(n).wait_send()
        int_relay(n).wait_send()
        int_onward(n).wait_send()

    @pl.loop(1, 16)
    def _(o):
        grad_zo(o).wait_send()

    @pl.loop(0, 16)
    def _(o):
        for j in (1, 2, 3):
            amp_y(o, j).wait_send()
        amp_c(o).wait_send()

    for k in range(4):
        for j in (1, 2, 3):
            int_x(k, j).wait_send()
            grad_yc(k, j).wait_send()
        grad_c(k).wait_send()
    for k in (1, 3):
        int_z(k).wait_send()
    for k in (1, 2, 3):
        dens_x(k).wait_send()
        dens_z(k).wait_send()


def local(i_list, pairs, vir_offsets, occ_energy, vir_energy, amplitudes, integrals):
    hbm = pl.BlockSpec(memory_space=pltpu.HBM)
    vmem = pl.BlockSpec(memory_space=pltpu.VMEM)
    dma = pltpu.SemaphoreType.DMA
    dens, grad = pl.pallas_call(
        kernel,
        out_shape=(
            jax.ShapeDtypeStruct((4, 64, 128), BF16),
            jax.ShapeDtypeStruct((2, 32, 64), BF16),
        ),
        in_specs=[hbm] * 8,
        out_specs=(vmem, vmem),
        scratch_shapes=[
            pltpu.SMEM((2,), jnp.int32), pltpu.SMEM((2, 2), jnp.int32),
            pltpu.SMEM((2,), jnp.int32), pltpu.SMEM((128,), F32), pltpu.SMEM((1024,), F32),
            pltpu.VMEM((8, 128), F32), pltpu.VMEM((2, 32, 64), BF16),
            pltpu.VMEM((2, 64, 2, 128), BF16), pltpu.VMEM((32, 128), BF16),
            pltpu.VMEM((4, 64, 128), BF16), dma((8,)),
            pltpu.VMEM((2, 32, 128), BF16), dma((2,)), dma((2,)),
            pltpu.VMEM((4, 4, 4, 2, 32, 128), BF16),
            pltpu.VMEM((16, 64, 128), BF16),
            pltpu.VMEM((4, 128, 128), BF16),
            pltpu.VMEM((4, 4, 4, 2, 32, 128), BF16),
            pltpu.VMEM((4, 4, 4, 32, 128), BF16),
            pltpu.VMEM((4, 4, 4, 32, 128), BF16),
            pltpu.VMEM((4, 4, 4, 32, 128), BF16),
            pltpu.VMEM((4, 4, 32, 128), BF16),
            pltpu.VMEM((16, 32, 128), BF16),
            pltpu.VMEM((4, 4, 64, 128), BF16),
            pltpu.VMEM((4, 4, 64, 128), BF16),
            pltpu.VMEM((4, 64, 128), BF16),
            pltpu.VMEM((4, 64, 128), BF16),
            dma((16,)), dma((16,)), dma((16, 4)), dma((16, 4)), dma((16,)), dma((16,)),
            dma((4,)), dma((4,)), dma((4, 4)), dma((4, 4)),
            dma((4,)), dma((4,)), dma((4,)), dma((4,)),
            dma((4,)), dma((4,)), dma((4, 4)), dma((4, 4)), dma((16,)), dma((16,)),
        ],
        compiler_params=pltpu.CompilerParams(collective_id=0, has_side_effects=True),
    )(
        i_list, pairs, vir_offsets, occ_energy, vir_energy, vir_energy.reshape(8, 128),
        amplitudes.transpose(0, 2, 1), integrals,
    )
    density = dens.reshape(2, 2, 64, 128).transpose(0, 2, 1, 3)
    return density, grad.transpose(0, 2, 1)


def solution(mesh):
    return jax.shard_map(
        local,
        mesh=mesh,
        in_specs=(P(), P(), P(), P(), P(), P(None, "row", "col"), P(None, "row", "col", None)),
        out_specs=(P(None, "row", "col", None), P(None, "row", "col")),
        check_vma=False,
    )
```

```python
import jax
import jax.numpy as jnp
from jax import lax
from jax.experimental import pallas as pl
from jax.experimental.pallas import tpu as pltpu
from jax.sharding import PartitionSpec as P

BF16 = jnp.bfloat16
F32 = jnp.float32
MESH = pl.DeviceIdType.MESH


def kernel(
    i_list, pairs, vir_offsets, occ_energy, vir_energy, vir_rows, amp_hbm, int_hbm,
    dens_out, grad_out,
    i_sm, pairs_sm, off_sm, occ_sm, vir_sm, vir_vm, amp_vm, int_vm, amp_in, int_in, in_sem, relay, ir_s, ir_r,
    amp, ints, ints_t, triples, scaled, grad, grad_core, grad_y, grad_yrecv, grad_z, grad_zrecv,
    grad_rel, dens, dens_xrecv, dens_sum, dens_zrecv, dens_all,
    az_s, az_r, ay_s, ay_r, ac_s, ac_r, iz_s, iz_r, ix_s, ix_r,
    dx_s, dx_r, dz_s, dz_r, gc_s, gc_r, gy_s, gy_r, gz_s, gz_r, gr_s, gr_r,
):
    row = lax.axis_index("row")
    col = lax.axis_index("col")
    x, zh = row // 4, row % 4
    zl, y, core = col // 8, (col // 2) % 4, col % 2
    z = zh * 4 + zl

    def z_peer(o):
        t = (z + o) % 16
        return (x * 4 + t // 4, (t % 4) * 8 + y * 2 + core)

    def zh_peer(k):
        return (x * 4 + (zh + k) % 4, col)

    def x_peer(j):
        return (((x + j) % 4) * 4 + zh, col)

    def y_peer(j):
        return (row, zl * 8 + ((y + j) % 4) * 2 + core)

    core_peer = (row, col + 1 - 2 * core)

    def remote(src, dst, ssem, rsem, dev):
        return pltpu.make_async_remote_copy(
            src_ref=src, dst_ref=dst, send_sem=ssem, recv_sem=rsem,
            device_id=dev, device_id_type=MESH,
        )

    loads = [
        pltpu.make_async_copy(src, dst, in_sem.at[n])
        for n, (src, dst) in enumerate((
            (amp_hbm, amp_vm), (int_hbm, int_vm), (vir_rows, vir_vm), (i_list, i_sm),
            (pairs, pairs_sm), (vir_offsets, off_sm), (occ_energy, occ_sm), (vir_energy, vir_sm),
        ))
    ]
    for load in loads:
        load.start()

    barrier = pltpu.get_barrier_semaphore()

    def greet(dev):
        pl.semaphore_signal(barrier, inc=1, device_id=dev, device_id_type=MESH)

    for o in (1, 2, 3, 4, 12, 13, 14, 15):
        greet(z_peer(o))
    for j in range(1, 4):
        greet(x_peer(j))
        greet(y_peer(j))
    greet(core_peer)
    loads[0].wait()
    amp_in[...] = jnp.concatenate([amp_vm[0], amp_vm[1]], axis=1)
    amp[zh, zl, y, core] = amp_in[...]
    pl.semaphore_wait(barrier, 15)

    def amp_z(o):
        return remote(amp_in, amp.at[zh, zl, y, core], az_s.at[o], az_r.at[o], z_peer(o))

    for o in (4, 12, 3, 13, 2, 14, 1, 15):
        amp_z(o).start()

    loads[1].wait()
    for i in range(2):
        v = int_vm[i].astype(F32)
        for b in range(2):
            int_in[2 * i + b] = v[:, b, :].astype(BF16)

    def int_z(k):
        return remote(int_in.at[(zh + k) % 4], ints.at[row], iz_s.at[k], iz_r.at[k], zh_peer(k))

    def int_relay(n):
        return remote(
            int_in.at[(zh + 2) % 4, pl.ds(32 * n, 32)], relay.at[n], ir_s.at[n], ir_r.at[n],
            zh_peer(1 + 2 * n),
        )

    def int_onward(n):
        k = 1 + 2 * n
        return remote(
            relay.at[n], ints.at[x * 4 + (zh + 4 - k) % 4, pl.ds(32 * n, 32)],
            iz_s.at[2 - 2 * n], iz_r.at[2 - 2 * n], zh_peer(k),
        )

    for n in range(2):
        int_relay(n).start()
    for k in (1, 3):
        int_z(k).start()

    ints[row] = int_in[zh]

    def amp_piece(o):
        s = (z - o + 16) % 16
        return s // 4, s % 4

    def amp_y(o, j):
        h, l = amp_piece(o)
        block = amp.at[h, l, y, core]
        return remote(block, block, ay_s.at[o, j], ay_r.at[o, j], y_peer(j))

    def amp_y_own(j):
        return remote(amp_in, amp.at[zh, zl, y, core], ay_s.at[0, j], ay_r.at[0, j], y_peer(j))

    def amp_c(o):
        h, l = amp_piece(o)
        block = amp.at[h, l, :, core]
        return remote(block, block, ac_s.at[o], ac_r.at[o], core_peer)

    def int_x(k, j):
        block = ints.at[x * 4 + (zh - k + 4) % 4]
        src = int_in.at[zh] if k == 0 else block
        return remote(src, block, ix_s.at[k, j], ix_r.at[k, j], x_peer(j))

    for j in (2, 1, 3):
        amp_y_own(j).start()
        int_x(0, j).start()

    for load in loads[2:]:
        load.wait()
    e_a = jnp.broadcast_to(vir_vm[pl.ds(off_sm[0] // 128, 1), :], (128, 128)).T
    e_b = vir_sm[off_sm[1] + col * 2 + zh % 2]
    e_i = occ_sm[i_sm[zh // 2]]
    occ0 = e_i + occ_sm[pairs_sm[0, 0]] + occ_sm[pairs_sm[0, 1]]
    occ1 = e_i + occ_sm[pairs_sm[1, 0]] + occ_sm[pairs_sm[1, 1]]
    first = lax.broadcasted_iota(jnp.int32, (1, 128), 1) < 64
    occ = jnp.where(first, occ0, occ1)
    row_part = []
    for h in range(4):
        e_c = vir_vm[pl.ds(x * 2 + h // 2, 1), :]
        turned = pltpu.roll(e_c, 64, axis=1)
        e_c = jnp.where(first, turned, e_c) if h % 2 else jnp.where(first, e_c, turned)
        row_part.append(occ - (e_c + e_b))

    def amp_on(o):
        near = 4 if o < 8 else 12
        h, l = amp_piece(near)
        block = amp.at[h, l, y, core]
        return remote(block, block, az_s.at[o], az_r.at[o], z_peer((o - near) % 16))

    def amp_half(n):
        near = 4 if n == 0 else 12
        h, l = amp_piece(near)
        block = amp.at[h, l, y, core, pl.ds(16 * n, 16)]
        return remote(block, block, az_s.at[8 - 8 * n], az_r.at[8 - 8 * n], z_peer(near))

    for o in (1, 15, 2, 14, 4, 12, 3, 13, 5, 11, 6, 10, 7, 9, 8):
        if o == 8:
            amp_half(0).wait_recv()
            amp_half(1).wait_recv()
        else:
            amp_z(o).wait_recv()
        if o == 4:
            amp_half(0).start()
            for t in (7, 6, 5):
                amp_on(t).start()
        if o == 12:
            amp_half(1).start()
            for t in (9, 10, 11):
                amp_on(t).start()
        for j in (2, 1, 3):
            amp_y(o, j).start()
        if o == 13:
            for n in range(2):
                int_relay(n).wait_recv()
                int_onward(n).start()
            for k in (1, 3):
                int_z(k).wait_recv()
                for j in (2, 1, 3):
                    int_x(k, j).start()

    for n in range(2):
        int_onward(n).wait_recv()
    for j in (2, 1, 3):
        int_x(2, j).start()

    for j in (1, 2, 3):
        amp_y_own(j).wait_recv()
    amp_c(0).start()

    for o in (1, 15, 2, 14, 4, 12, 3, 13, 5, 11, 6, 10, 7, 9, 8):
        for j in (1, 2, 3):
            amp_y(o, j).wait_recv()
        amp_c(o).start()

    for k in (0, 1, 3, 2):
        for j in (1, 2, 3):
            int_x(k, j).wait_recv()
    for l in range(4):
        ints_t[l] = ints[4 * l:4 * l + 4].reshape(256, 128).T
    triples[...] = jnp.zeros_like(triples)

    for o in (0, 1, 15, 2, 14, 4, 12, 3, 13, 5, 11, 6, 10, 7, 9, 8):
        amp_c(o).wait_recv()
        h, l = amp_piece(o)
        triples[h] += jnp.dot(
            ints_t[l], amp[h, l].reshape(256, 128), preferred_element_type=F32
        )
    for h in range(4):
        scaled[h] = (triples[h] / (row_part[h] - e_a)).astype(BF16)

    def grad_c(o):
        t = (z + o) % 16
        return remote(
            grad.at[t, :, 1 - core], grad_core.at[o], gc_s.at[o], gc_r.at[o], core_peer
        )

    def grad_dot(o):
        t = (z + o) % 16
        rows = ints[pl.ds((t % 4) * 4, 4)].reshape(256, 128)
        g = jnp.dot(rows, scaled[t // 4], preferred_element_type=F32)
        grad[t] = g.astype(BF16).reshape(4, 2, 32, 128)
        grad_c(o).start()

    far = (8, 7, 9, 6, 10, 5, 11)
    near = (3, 13, 2, 14, 1, 15)
    for o in far:
        grad_dot(o)

    def dens_x(k, j):
        return remote(
            dens.at[(x + j) % 4, (zh + k) % 4], dens_xrecv.at[k, j], dx_s.at[k, j],
            dx_r.at[k, j], x_peer(j),
        )

    for j in (2, 1, 3, 0):
        t = (x + j) % 4
        acc = jnp.zeros((256, 128), F32)
        for h in range(4):
            acc += lax.dot_general(
                amp[h, t].reshape(256, 128), scaled[h], (((1,), (1,)), ((), ())),
                preferred_element_type=F32,
            )
        dens[t] = acc.astype(BF16).reshape(4, 64, 128)
    for k in (2, 1, 3, 0):
        for j in (2, 1, 3):
            dens_x(k, j).start()

    def grad_yc(o, j):
        return remote(
            grad_y.at[o, (y + j) % 4], grad_yrecv.at[o, j], gy_s.at[o, j], gy_r.at[o, j],
            y_peer(j),
        )

    def core_sum(o):
        grad_c(o).wait_recv()
        v = grad[(z + o) % 16, :, core].astype(F32) + grad_core[o].astype(F32)
        grad_y[o] = v.astype(BF16)
        for j in (2, 1, 3):
            grad_yc(o, j).start()

    for o in far:
        core_sum(o)
    for o in (4, 12) + near + (0,):
        grad_dot(o)

    def dens_z(k):
        return remote(
            dens_sum.at[(zh + k) % 4], dens_zrecv.at[k], dz_s.at[k], dz_r.at[k], zh_peer(k)
        )

    def dens_add(k):
        h = (zh + k) % 4
        total = dens[x, h].astype(F32)
        for j in (1, 3, 2):
            dens_x(k, j).wait_recv()
            total += dens_xrecv[k, j].astype(F32)
        dens_sum[h] = total.astype(BF16)
        if k:
            dens_z(k).start()

    dens_add(2)
    for o in (4, 12) + near + (0,):
        core_sum(o)
    dens_add(1)
    dens_add(3)

    def y_sum(o):
        v = grad_y[o, y].astype(F32)
        for j in (1, 3, 2):
            grad_yc(o, j).wait_recv()
            v += grad_yrecv[o, j].astype(F32)
        return v

    def grad_zc(o):
        return remote(
            grad_z.at[o], grad_zrecv.at[o], gz_s.at[o], gz_r.at[o], z_peer(o)
        )

    def grad_r(n, m):
        o = 5 + m if n == 0 else 11 - m
        if m < 3:
            src, dst = grad_z.at[o], grad_rel.at[n, m]
        else:
            half = pl.ds(16 * n, 16)
            src, dst = grad_z.at[8, half], grad_rel.at[n, 3, half]
        return remote(
            src, dst, gr_s.at[n, m], gr_r.at[n, m], z_peer(1 + m if n == 0 else 15 - m)
        )

    for o in far:
        grad_z[o] = y_sum(o).astype(BF16)
        if o == 8:
            grad_r(0, 3).start()
            grad_r(1, 3).start()
        elif o < 8:
            grad_r(0, o - 5).start()
        else:
            grad_r(1, 11 - o).start()
    dens_add(0)
    for o in near:
        grad_z[o] = y_sum(o).astype(BF16)
        grad_zc(o).start()
    for n in range(2):
        o = 4 if n == 0 else 12
        v = y_sum(o)
        for m in range(4):
            grad_r(n, m).wait_recv()
        for m in range(3):
            v += grad_rel[n, m].astype(F32)
        half = slice(16 * n, 16 * n + 16)
        rest = slice(16 - 16 * n, 32 - 16 * n)
        grad_z[o, half] = (v[half] + grad_rel[n, 3, half].astype(F32)).astype(BF16)
        grad_z[o, rest] = v[rest].astype(BF16)
        grad_zc(o).start()
    total = y_sum(0)

    for k in (1, 3, 2):
        dens_z(k).wait_recv()
        dens_all[(zh - k + 4) % 4] = dens_zrecv[k]
    dens_all[zh] = dens_sum[zh]
    for i in range(2):
        dens_out[i] = jnp.stack(
            [dens_all[2 * i].astype(F32), dens_all[2 * i + 1].astype(F32)], axis=1
        ).astype(BF16)

    for o in near + (4, 12):
        grad_zc(o).wait_recv()
        total += grad_zrecv[o].astype(F32)
    grad_out[0] = total[:, :64].astype(BF16)
    grad_out[1] = total[:, 64:].astype(BF16)

    for o in (1, 2, 3, 4, 5, 6, 7, 9, 10, 11, 12, 13, 14, 15):
        amp_z(o).wait_send()
    for n in range(2):
        amp_half(n).wait_send()
        int_relay(n).wait_send()
        int_onward(n).wait_send()

    for o in near + (4, 12):
        grad_zc(o).wait_send()
    for n in range(2):
        for m in range(4):
            grad_r(n, m).wait_send()

    @pl.loop(0, 16)
    def _(o):
        for j in (1, 2, 3):
            amp_y(o, j).wait_send()
            grad_yc(o, j).wait_send()
        amp_c(o).wait_send()
        grad_c(o).wait_send()

    for k in range(4):
        for j in (1, 2, 3):
            int_x(k, j).wait_send()
            dens_x(k, j).wait_send()
    for k in (1, 3):
        int_z(k).wait_send()
    for k in (1, 2, 3):
        dens_z(k).wait_send()


def local(i_list, pairs, vir_offsets, occ_energy, vir_energy, amplitudes, integrals):
    hbm = pl.BlockSpec(memory_space=pltpu.HBM)
    vmem = pl.BlockSpec(memory_space=pltpu.VMEM)
    dma = pltpu.SemaphoreType.DMA
    dens, grad = pl.pallas_call(
        kernel,
        out_shape=(
            jax.ShapeDtypeStruct((2, 64, 2, 128), BF16),
            jax.ShapeDtypeStruct((2, 32, 64), BF16),
        ),
        in_specs=[hbm] * 8,
        out_specs=(vmem, vmem),
        scratch_shapes=[
            pltpu.SMEM((2,), jnp.int32), pltpu.SMEM((2, 2), jnp.int32),
            pltpu.SMEM((2,), jnp.int32), pltpu.SMEM((128,), F32), pltpu.SMEM((1024,), F32),
            pltpu.VMEM((8, 128), F32), pltpu.VMEM((2, 32, 64), BF16),
            pltpu.VMEM((2, 64, 2, 128), BF16), pltpu.VMEM((32, 128), BF16),
            pltpu.VMEM((4, 64, 128), BF16), dma((8,)),
            pltpu.VMEM((2, 32, 128), BF16), dma((2,)), dma((2,)),
            pltpu.VMEM((4, 4, 4, 2, 32, 128), BF16),
            pltpu.VMEM((16, 64, 128), BF16),
            pltpu.VMEM((4, 128, 256), BF16),
            pltpu.VMEM((4, 128, 128), F32),
            pltpu.VMEM((4, 128, 128), BF16),
            pltpu.VMEM((16, 4, 2, 32, 128), BF16),
            pltpu.VMEM((16, 4, 32, 128), BF16),
            pltpu.VMEM((16, 4, 32, 128), BF16),
            pltpu.VMEM((16, 4, 32, 128), BF16),
            pltpu.VMEM((16, 32, 128), BF16),
            pltpu.VMEM((16, 32, 128), BF16),
            pltpu.VMEM((2, 4, 32, 128), BF16),
            pltpu.VMEM((4, 4, 64, 128), BF16),
            pltpu.VMEM((4, 4, 64, 128), BF16),
            pltpu.VMEM((4, 64, 128), BF16),
            pltpu.VMEM((4, 64, 128), BF16),
            pltpu.VMEM((4, 64, 128), BF16),
            dma((16,)), dma((16,)), dma((16, 4)), dma((16, 4)), dma((16,)), dma((16,)),
            dma((4,)), dma((4,)), dma((4, 4)), dma((4, 4)),
            dma((4, 4)), dma((4, 4)), dma((4,)), dma((4,)),
            dma((16,)), dma((16,)), dma((16, 4)), dma((16, 4)), dma((16,)), dma((16,)),
            dma((2, 4)), dma((2, 4)),
        ],
        compiler_params=pltpu.CompilerParams(collective_id=0, has_side_effects=True),
    )(
        i_list, pairs, vir_offsets, occ_energy, vir_energy, vir_energy.reshape(8, 128),
        amplitudes.transpose(0, 2, 1), integrals,
    )
    return dens, grad.transpose(0, 2, 1)


def solution(mesh):
    return jax.shard_map(
        local,
        mesh=mesh,
        in_specs=(P(), P(), P(), P(), P(), P(None, "row", "col"), P(None, "row", "col", None)),
        out_specs=(P(None, "row", "col", None), P(None, "row", "col")),
        check_vma=False,
    )
```

```python
import jax
import jax.numpy as jnp
from jax import lax
from jax.experimental import pallas as pl
from jax.experimental.pallas import tpu as pltpu
from jax.sharding import PartitionSpec as P

BF16 = jnp.bfloat16
F32 = jnp.float32
MESH = pl.DeviceIdType.MESH


def kernel(
    i_list, pairs, vir_offsets, occ_energy, vir_energy, vir_rows, amp_hbm, int_hbm,
    dens_out, grad_out,
    i_sm, pairs_sm, off_sm, occ_sm, vir_sm, vir_vm, amp_vm, int_vm, amp_in, int_in, in_sem, relay, ir_s, ir_r,
    amp, ints, scaled, grad, grad_core, grad_y, grad_yrecv, grad_z, grad_zrecv,
    dens, dens_xrecv, dens_sum, dens_zrecv,
    az_s, az_r, ay_s, ay_r, ac_s, ac_r, iz_s, iz_r, ix_s, ix_r,
    dx_s, dx_r, dz_s, dz_r, gc_s, gc_r, gy_s, gy_r, gz_s, gz_r,
):
    row = lax.axis_index("row")
    col = lax.axis_index("col")
    x, zh = row // 4, row % 4
    zl, y, core = col // 8, (col // 2) % 4, col % 2
    z = zh * 4 + zl

    def z_peer(o):
        t = (z + o) % 16
        return (x * 4 + t // 4, (t % 4) * 8 + y * 2 + core)

    def zh_peer(k):
        return (x * 4 + (zh + k) % 4, col)

    def x_peer(j):
        return (((x + j) % 4) * 4 + zh, col)

    def y_peer(j):
        return (row, zl * 8 + ((y + j) % 4) * 2 + core)

    core_peer = (row, col + 1 - 2 * core)

    def remote(src, dst, ssem, rsem, dev):
        return pltpu.make_async_remote_copy(
            src_ref=src, dst_ref=dst, send_sem=ssem, recv_sem=rsem,
            device_id=dev, device_id_type=MESH,
        )

    loads = [
        pltpu.make_async_copy(src, dst, in_sem.at[n])
        for n, (src, dst) in enumerate((
            (amp_hbm, amp_vm), (int_hbm, int_vm), (vir_rows, vir_vm), (i_list, i_sm),
            (pairs, pairs_sm), (vir_offsets, off_sm), (occ_energy, occ_sm), (vir_energy, vir_sm),
        ))
    ]
    for load in loads:
        load.start()

    barrier = pltpu.get_barrier_semaphore()

    def greet(dev):
        pl.semaphore_signal(barrier, inc=1, device_id=dev, device_id_type=MESH)

    for o in (1, 2, 3, 4, 12, 13, 14, 15):
        greet(z_peer(o))
    for j in range(1, 4):
        greet(x_peer(j))
        greet(y_peer(j))
    greet(core_peer)
    loads[0].wait()
    amp_in[...] = jnp.concatenate([amp_vm[0], amp_vm[1]], axis=1)
    amp[zh, zl, y, core] = amp_in[...]
    pl.semaphore_wait(barrier, 15)

    def amp_z(o):
        return remote(amp_in, amp.at[zh, zl, y, core], az_s.at[o], az_r.at[o], z_peer(o))

    for o in (4, 12, 3, 13, 2, 14, 1, 15):
        amp_z(o).start()

    loads[1].wait()
    for i in range(2):
        v = int_vm[i].astype(F32)
        for b in range(2):
            int_in[2 * i + b] = v[:, b, :].astype(BF16)

    def int_z(k):
        return remote(int_in.at[(zh + k) % 4], ints.at[row], iz_s.at[k], iz_r.at[k], zh_peer(k))

    def int_relay(n):
        return remote(
            int_in.at[(zh + 2) % 4, pl.ds(32 * n, 32)], relay.at[n], ir_s.at[n], ir_r.at[n],
            zh_peer(1 + 2 * n),
        )

    def int_onward(n):
        k = 1 + 2 * n
        return remote(
            relay.at[n], ints.at[x * 4 + (zh + 4 - k) % 4, pl.ds(32 * n, 32)],
            iz_s.at[2 - 2 * n], iz_r.at[2 - 2 * n], zh_peer(k),
        )

    for n in range(2):
        int_relay(n).start()
    for k in (1, 3):
        int_z(k).start()

    ints[row] = int_in[zh]

    def amp_piece(o):
        s = (z - o + 16) % 16
        return s // 4, s % 4

    def amp_y(o, j):
        h, l = amp_piece(o)
        block = amp.at[h, l, y, core]
        return remote(block, block, ay_s.at[o, j], ay_r.at[o, j], y_peer(j))

    def amp_y_own(j):
        return remote(amp_in, amp.at[zh, zl, y, core], ay_s.at[0, j], ay_r.at[0, j], y_peer(j))

    def amp_c(o):
        h, l = amp_piece(o)
        block = amp.at[h, l, :, core]
        return remote(block, block, ac_s.at[o], ac_r.at[o], core_peer)

    def int_x(k, j):
        block = ints.at[x * 4 + (zh - k + 4) % 4]
        src = int_in.at[zh] if k == 0 else block
        return remote(src, block, ix_s.at[k, j], ix_r.at[k, j], x_peer(j))

    for j in (2, 1, 3):
        amp_y_own(j).start()
        int_x(0, j).start()

    for load in loads[2:]:
        load.wait()
    e_a = jnp.broadcast_to(vir_vm[pl.ds(off_sm[0] // 128, 1), :], (128, 128)).T
    e_b = vir_sm[off_sm[1] + col * 2 + zh % 2]
    e_i = occ_sm[i_sm[zh // 2]]
    occ0 = e_i + occ_sm[pairs_sm[0, 0]] + occ_sm[pairs_sm[0, 1]]
    occ1 = e_i + occ_sm[pairs_sm[1, 0]] + occ_sm[pairs_sm[1, 1]]
    first = lax.broadcasted_iota(jnp.int32, (1, 128), 1) < 64
    occ = jnp.where(first, occ0, occ1)
    row_part = []
    for h in range(4):
        e_c = vir_vm[pl.ds(x * 2 + h // 2, 1), :]
        turned = pltpu.roll(e_c, 64, axis=1)
        e_c = jnp.where(first, turned, e_c) if h % 2 else jnp.where(first, e_c, turned)
        row_part.append(occ - (e_c + e_b))

    def amp_on(o):
        near = 4 if o < 8 else 12
        h, l = amp_piece(near)
        block = amp.at[h, l, y, core]
        return remote(block, block, az_s.at[o], az_r.at[o], z_peer((o - near) % 16))

    def amp_half(n):
        near = 4 if n == 0 else 12
        h, l = amp_piece(near)
        block = amp.at[h, l, y, core, pl.ds(16 * n, 16)]
        return remote(block, block, az_s.at[8 - 8 * n], az_r.at[8 - 8 * n], z_peer(near))

    for o in (1, 15, 2, 14, 4, 12, 3, 13, 5, 11, 6, 10, 7, 9, 8):
        if o == 8:
            amp_half(0).wait_recv()
            amp_half(1).wait_recv()
        else:
            amp_z(o).wait_recv()
        if o == 4:
            amp_half(0).start()
            for t in (7, 6, 5):
                amp_on(t).start()
        if o == 12:
            amp_half(1).start()
            for t in (9, 10, 11):
                amp_on(t).start()
        for j in (2, 1, 3):
            amp_y(o, j).start()
        if o == 13:
            for n in range(2):
                int_relay(n).wait_recv()
                int_onward(n).start()
            for k in (1, 3):
                int_z(k).wait_recv()
                for j in (2, 1, 3):
                    int_x(k, j).start()

    for n in range(2):
        int_onward(n).wait_recv()
    for j in (2, 1, 3):
        int_x(2, j).start()

    for j in (1, 2, 3):
        amp_y_own(j).wait_recv()
    amp_c(0).start()

    for o in (1, 15, 2, 14, 4, 12, 3, 13, 5, 11, 6, 10, 7, 9, 8):
        for j in (1, 2, 3):
            amp_y(o, j).wait_recv()
        amp_c(o).start()

    for k in (0, 1, 3, 2):
        for j in (1, 2, 3):
            int_x(k, j).wait_recv()
    ints_all = ints[...].reshape(1024, 128)
    ints_t = ints_all.T

    @pl.loop(0, 16)
    def _(o):
        amp_c(o).wait_recv()

    for h in range(4):
        t = jnp.dot(ints_t, amp[h].reshape(1024, 128), preferred_element_type=F32)
        scaled[h] = (t / (row_part[h] - e_a)).astype(BF16)

    def dens_x(k, j):
        return remote(
            dens.at[(x + j) % 4, (zh + k) % 4], dens_xrecv.at[k, j], dx_s.at[k, j],
            dx_r.at[k, j], x_peer(j),
        )

    for j in (2, 1, 3, 0):
        t = (x + j) % 4
        acc = jnp.zeros((256, 128), F32)
        for h in range(4):
            acc += lax.dot_general(
                amp[h, t].reshape(256, 128), scaled[h], (((1,), (1,)), ((), ())),
                preferred_element_type=F32,
            )
        dens[t] = acc.astype(BF16).reshape(4, 64, 128)
    for k in (2, 1, 3, 0):
        for j in (2, 1, 3):
            dens_x(k, j).start()

    def grad_c(h):
        return remote(
            grad.at[h, :, :, 1 - core], grad_core.at[h], gc_s.at[h], gc_r.at[h], core_peer
        )

    for k in (2, 1, 3, 0):
        h = (zh + k) % 4
        g = jnp.dot(ints_all, scaled[h], preferred_element_type=F32)
        grad[h] = g.astype(BF16).reshape(4, 4, 2, 32, 128)
        grad_c(h).start()

    def dens_z(k):
        return remote(
            dens_sum.at[(zh + k) % 4], dens_zrecv.at[k], dz_s.at[k], dz_r.at[k], zh_peer(k)
        )

    def dens_add(k):
        h = (zh + k) % 4
        total = dens[x, h].astype(F32)
        for j in (1, 3, 2):
            dens_x(k, j).wait_recv()
            total += dens_xrecv[k, j].astype(F32)
        dens_sum[h] = total.astype(BF16)
        if k:
            dens_z(k).start()

    def grad_yc(k, j):
        h = (zh + k) % 4
        return remote(
            grad_y.at[h, :, (y + j) % 4], grad_yrecv.at[k, j], gy_s.at[k, j], gy_r.at[k, j],
            y_peer(j),
        )

    for k in (2, 1, 3, 0):
        h = (zh + k) % 4
        grad_c(h).wait_recv()
        s = grad[h, :, :, core].astype(F32) + grad_core[h].astype(F32)
        grad_y[h] = s.astype(BF16)
        for j in (2, 1, 3):
            grad_yc(k, j).start()

    for k in (2, 1, 3, 0):
        dens_add(k)

    def grad_zc(k, m):
        t = (zl + m) % 4
        o = (4 * k + t - zl + 16) % 16
        return remote(
            grad_z.at[(zh + k) % 4, t], grad_zrecv.at[o], gz_s.at[o], gz_r.at[o], z_peer(o)
        )

    for k in (2, 1, 3, 0):
        h = (zh + k) % 4
        s = grad_y[h, :, y].astype(F32)
        for j in (1, 3, 2):
            grad_yc(k, j).wait_recv()
            s += grad_yrecv[k, j].astype(F32)
        grad_z[h] = s.astype(BF16)
        for m in range(4):
            if k or m:
                grad_zc(k, m).start()

    dens_out[zh] = dens_sum[zh]
    for k in (1, 3, 2):
        dens_z(k).wait_recv()
        dens_out[(zh - k + 4) % 4] = dens_zrecv[k]

    def grad_zo(o):
        return remote(
            grad_z.at[0, 0], grad_zrecv.at[o], gz_s.at[o], gz_r.at[o], z_peer(o)
        )

    def add_z(o, s):
        grad_zo(o).wait_recv()
        return s + grad_zrecv[o].astype(F32)

    s = lax.fori_loop(1, 16, add_z, grad_z[zh, zl].astype(F32))
    grad_out[0] = s[:, :64].astype(BF16)
    grad_out[1] = s[:, 64:].astype(BF16)

    for o in (1, 2, 3, 4, 5, 6, 7, 9, 10, 11, 12, 13, 14, 15):
        amp_z(o).wait_send()
    for n in range(2):
        amp_half(n).wait_send()
        int_relay(n).wait_send()
        int_onward(n).wait_send()

    @pl.loop(1, 16)
    def _(o):
        grad_zo(o).wait_send()

    @pl.loop(0, 16)
    def _(o):
        for j in (1, 2, 3):
            amp_y(o, j).wait_send()
        amp_c(o).wait_send()

    for k in range(4):
        for j in (1, 2, 3):
            int_x(k, j).wait_send()
            grad_yc(k, j).wait_send()
            dens_x(k, j).wait_send()
        grad_c(k).wait_send()
    for k in (1, 3):
        int_z(k).wait_send()
    for k in (1, 2, 3):
        dens_z(k).wait_send()


def local(i_list, pairs, vir_offsets, occ_energy, vir_energy, amplitudes, integrals):
    hbm = pl.BlockSpec(memory_space=pltpu.HBM)
    vmem = pl.BlockSpec(memory_space=pltpu.VMEM)
    dma = pltpu.SemaphoreType.DMA
    dens, grad = pl.pallas_call(
        kernel,
        out_shape=(
            jax.ShapeDtypeStruct((4, 64, 128), BF16),
            jax.ShapeDtypeStruct((2, 32, 64), BF16),
        ),
        in_specs=[hbm] * 8,
        out_specs=(vmem, vmem),
        scratch_shapes=[
            pltpu.SMEM((2,), jnp.int32), pltpu.SMEM((2, 2), jnp.int32),
            pltpu.SMEM((2,), jnp.int32), pltpu.SMEM((128,), F32), pltpu.SMEM((1024,), F32),
            pltpu.VMEM((8, 128), F32), pltpu.VMEM((2, 32, 64), BF16),
            pltpu.VMEM((2, 64, 2, 128), BF16), pltpu.VMEM((32, 128), BF16),
            pltpu.VMEM((4, 64, 128), BF16), dma((8,)),
            pltpu.VMEM((2, 32, 128), BF16), dma((2,)), dma((2,)),
            pltpu.VMEM((4, 4, 4, 2, 32, 128), BF16),
            pltpu.VMEM((16, 64, 128), BF16),
            pltpu.VMEM((4, 128, 128), BF16),
            pltpu.VMEM((4, 4, 4, 2, 32, 128), BF16),
            pltpu.VMEM((4, 4, 4, 32, 128), BF16),
            pltpu.VMEM((4, 4, 4, 32, 128), BF16),
            pltpu.VMEM((4, 4, 4, 32, 128), BF16),
            pltpu.VMEM((4, 4, 32, 128), BF16),
            pltpu.VMEM((16, 32, 128), BF16),
            pltpu.VMEM((4, 4, 64, 128), BF16),
            pltpu.VMEM((4, 4, 64, 128), BF16),
            pltpu.VMEM((4, 64, 128), BF16),
            pltpu.VMEM((4, 64, 128), BF16),
            dma((16,)), dma((16,)), dma((16, 4)), dma((16, 4)), dma((16,)), dma((16,)),
            dma((4,)), dma((4,)), dma((4, 4)), dma((4, 4)),
            dma((4, 4)), dma((4, 4)), dma((4,)), dma((4,)),
            dma((4,)), dma((4,)), dma((4, 4)), dma((4, 4)), dma((16,)), dma((16,)),
        ],
        compiler_params=pltpu.CompilerParams(collective_id=0, has_side_effects=True, vmem_limit_bytes=24 << 20),
    )(
        *(
            pltpu.with_memory_space_constraint(v, pltpu.HBM)
            for v in (
                i_list, pairs, vir_offsets, occ_energy, vir_energy, vir_energy.reshape(8, 128),
                amplitudes.transpose(0, 2, 1), integrals,
            )
        )
    )
    density = dens.reshape(2, 2, 64, 128).transpose(0, 2, 1, 3)
    return density, grad.transpose(0, 2, 1)


def solution(mesh):
    return jax.shard_map(
        local,
        mesh=mesh,
        in_specs=(P(), P(), P(), P(), P(), P(None, "row", "col"), P(None, "row", "col", None)),
        out_specs=(P(None, "row", "col", None), P(None, "row", "col")),
        check_vma=False,
    )
```

```python
import jax
import jax.numpy as jnp
from jax import lax
from jax.experimental import pallas as pl
from jax.experimental.pallas import tpu as pltpu
from jax.sharding import PartitionSpec as P

BF16 = jnp.bfloat16
F32 = jnp.float32
MESH = pl.DeviceIdType.MESH


def kernel(
    i_list, pairs, vir_offsets, occ_energy, vir_energy, vir_rows, amp_hbm, int_hbm,
    dens_out, grad_out,
    i_sm, pairs_sm, off_sm, occ_sm, vir_sm, vir_vm, amp_vm, int_vm, amp_in, int_in, in_sem, relay, ir_s, ir_r,
    amp, ints, scaled, grad, grad_core, grad_y, grad_yrecv, grad_z, grad_zrecv,
    dens, dens_xrecv, dens_sum, dens_zrecv,
    az_s, az_r, ay_s, ay_r, ac_s, ac_r, iz_s, iz_r, ix_s, ix_r,
    dx_s, dx_r, dz_s, dz_r, gc_s, gc_r, gy_s, gy_r, gz_s, gz_r,
):
    row = lax.axis_index("row")
    col = lax.axis_index("col")
    x, zh = row // 4, row % 4
    zl, y, core = col // 8, (col // 2) % 4, col % 2
    z = zh * 4 + zl

    def z_peer(o):
        t = (z + o) % 16
        return (x * 4 + t // 4, (t % 4) * 8 + y * 2 + core)

    def zh_peer(k):
        return (x * 4 + (zh + k) % 4, col)

    def x_peer(j):
        return (((x + j) % 4) * 4 + zh, col)

    def y_peer(j):
        return (row, zl * 8 + ((y + j) % 4) * 2 + core)

    core_peer = (row, col + 1 - 2 * core)

    def remote(src, dst, ssem, rsem, dev):
        return pltpu.make_async_remote_copy(
            src_ref=src, dst_ref=dst, send_sem=ssem, recv_sem=rsem,
            device_id=dev, device_id_type=MESH,
        )

    loads = [
        pltpu.make_async_copy(src, dst, in_sem.at[n])
        for n, (src, dst) in enumerate((
            (amp_hbm, amp_vm), (int_hbm, int_vm), (vir_rows, vir_vm), (i_list, i_sm),
            (pairs, pairs_sm), (vir_offsets, off_sm), (occ_energy, occ_sm), (vir_energy, vir_sm),
        ))
    ]
    barrier = pltpu.get_barrier_semaphore()

    def greet(dev):
        pl.semaphore_signal(barrier, inc=1, device_id=dev, device_id_type=MESH)

    loads[0].start()
    for o in (4, 12, 3, 13, 2, 14, 1, 15):
        greet(z_peer(o))
    for j in range(1, 4):
        greet(x_peer(j))
        greet(y_peer(j))
    greet(core_peer)
    for load in loads[1:]:
        load.start()
    loads[0].wait()
    amp_in[...] = jnp.concatenate([amp_vm[0], amp_vm[1]], axis=1)
    amp[zh, zl, y, core] = amp_in[...]
    pl.semaphore_wait(barrier, 15)

    def amp_z(o):
        return remote(amp_in, amp.at[zh, zl, y, core], az_s.at[o], az_r.at[o], z_peer(o))

    for o in (4, 12, 3, 13, 2, 14, 1, 15):
        amp_z(o).start()

    loads[1].wait()
    for i in range(2):
        v = int_vm[i].astype(F32)
        for b in range(2):
            int_in[2 * i + b] = v[:, b, :].astype(BF16)

    def int_z(k):
        return remote(int_in.at[(zh + k) % 4], ints.at[row], iz_s.at[k], iz_r.at[k], zh_peer(k))

    def int_relay(n):
        return remote(
            int_in.at[(zh + 2) % 4, pl.ds(32 * n, 32)], relay.at[n], ir_s.at[n], ir_r.at[n],
            zh_peer(1 + 2 * n),
        )

    def int_onward(n):
        k = 1 + 2 * n
        return remote(
            relay.at[n], ints.at[x * 4 + (zh + 4 - k) % 4, pl.ds(32 * n, 32)],
            iz_s.at[2 - 2 * n], iz_r.at[2 - 2 * n], zh_peer(k),
        )

    for n in range(2):
        int_relay(n).start()
    for k in (1, 3):
        int_z(k).start()

    ints[row] = int_in[zh]

    def amp_piece(o):
        s = (z - o + 16) % 16
        return s // 4, s % 4

    def amp_y(o, j):
        h, l = amp_piece(o)
        block = amp.at[h, l, y, core]
        return remote(block, block, ay_s.at[o, j], ay_r.at[o, j], y_peer(j))

    def amp_y_own(j):
        return remote(amp_in, amp.at[zh, zl, y, core], ay_s.at[0, j], ay_r.at[0, j], y_peer(j))

    def amp_c(o):
        h, l = amp_piece(o)
        block = amp.at[h, l, :, core]
        return remote(block, block, ac_s.at[o], ac_r.at[o], core_peer)

    def int_x(k, j):
        block = ints.at[x * 4 + (zh - k + 4) % 4]
        src = int_in.at[zh] if k == 0 else block
        return remote(src, block, ix_s.at[k, j], ix_r.at[k, j], x_peer(j))

    for j in (2, 1, 3):
        amp_y_own(j).start()
        int_x(0, j).start()

    for load in loads[2:]:
        load.wait()
    e_a = jnp.broadcast_to(vir_vm[pl.ds(off_sm[0] // 128, 1), :], (128, 128)).T
    e_b = vir_sm[off_sm[1] + col * 2 + zh % 2]
    e_i = occ_sm[i_sm[zh // 2]]
    occ0 = e_i + occ_sm[pairs_sm[0, 0]] + occ_sm[pairs_sm[0, 1]]
    occ1 = e_i + occ_sm[pairs_sm[1, 0]] + occ_sm[pairs_sm[1, 1]]
    first = lax.broadcasted_iota(jnp.int32, (1, 128), 1) < 64
    occ = jnp.where(first, occ0, occ1)
    row_part = []
    for h in range(4):
        e_c = vir_vm[pl.ds(x * 2 + h // 2, 1), :]
        turned = pltpu.roll(e_c, 64, axis=1)
        e_c = jnp.where(first, turned, e_c) if h % 2 else jnp.where(first, e_c, turned)
        row_part.append(occ - (e_c + e_b))

    def amp_on(o):
        near = 4 if o < 8 else 12
        h, l = amp_piece(near)
        block = amp.at[h, l, y, core]
        return remote(block, block, az_s.at[o], az_r.at[o], z_peer((o - near) % 16))

    def amp_half(n):
        near = 4 if n == 0 else 12
        h, l = amp_piece(near)
        block = amp.at[h, l, y, core, pl.ds(16 * n, 16)]
        return remote(block, block, az_s.at[8 - 8 * n], az_r.at[8 - 8 * n], z_peer(near))

    for o in (1, 15, 2, 14, 4, 12, 3, 13, 5, 11, 6, 10, 7, 9, 8):
        if o == 8:
            amp_half(0).wait_recv()
            amp_half(1).wait_recv()
        else:
            amp_z(o).wait_recv()
        if o == 4:
            amp_half(0).start()
            for t in (7, 6, 5):
                amp_on(t).start()
        if o == 12:
            amp_half(1).start()
            for t in (9, 10, 11):
                amp_on(t).start()
        for j in (2, 1, 3):
            amp_y(o, j).start()
        if o == 13:
            for n in range(2):
                int_relay(n).wait_recv()
                int_onward(n).start()
            for k in (1, 3):
                int_z(k).wait_recv()
                for j in (2, 1, 3):
                    int_x(k, j).start()

    for n in range(2):
        int_onward(n).wait_recv()
    for j in (2, 1, 3):
        int_x(2, j).start()

    for j in (1, 2, 3):
        amp_y_own(j).wait_recv()
    amp_c(0).start()

    for o in (1, 15, 2, 14, 4, 12, 3, 13, 5, 11, 6, 10, 7, 9, 8):
        for j in (1, 2, 3):
            amp_y(o, j).wait_recv()
        amp_c(o).start()

    for k in (0, 1, 3, 2):
        for j in (1, 2, 3):
            int_x(k, j).wait_recv()
    ints_all = ints[...].reshape(1024, 128)
    ints_t = ints_all.T

    @pl.loop(0, 16)
    def _(o):
        amp_c(o).wait_recv()

    for h in range(4):
        t = jnp.dot(ints_t, amp[h].reshape(1024, 128), preferred_element_type=F32)
        scaled[h] = (t / (row_part[h] - e_a)).astype(BF16)

    def grad_c(h):
        return remote(
            grad.at[h, :, :, 1 - core], grad_core.at[h], gc_s.at[h], gc_r.at[h], core_peer
        )

    def grad_dot(k):
        h = (zh + k) % 4
        g = jnp.dot(ints_all, scaled[h], preferred_element_type=F32)
        grad[h] = g.astype(BF16).reshape(4, 4, 2, 32, 128)
        grad_c(h).start()

    grad_dot(2)

    def dens_x(k, j):
        return remote(
            dens.at[(x + j) % 4, (zh + k) % 4], dens_xrecv.at[k, j], dx_s.at[k, j],
            dx_r.at[k, j], x_peer(j),
        )

    for j in (2, 1, 3, 0):
        t = (x + j) % 4
        acc = jnp.zeros((256, 128), F32)
        for h in range(4):
            acc += lax.dot_general(
                amp[h, t].reshape(256, 128), scaled[h], (((1,), (1,)), ((), ())),
                preferred_element_type=F32,
            )
        dens[t] = acc.astype(BF16).reshape(4, 64, 128)
    for k in (2, 1, 3, 0):
        for j in (2, 1, 3):
            dens_x(k, j).start()

    for k in (1, 3, 0):
        grad_dot(k)

    def dens_z(k):
        return remote(
            dens_sum.at[(zh + k) % 4], dens_zrecv.at[k], dz_s.at[k], dz_r.at[k], zh_peer(k)
        )

    def dens_add(k):
        h = (zh + k) % 4
        total = dens[x, h].astype(F32)
        for j in (1, 3, 2):
            dens_x(k, j).wait_recv()
            total += dens_xrecv[k, j].astype(F32)
        dens_sum[h] = total.astype(BF16)
        if k:
            dens_z(k).start()

    def grad_yc(k, j):
        h = (zh + k) % 4
        return remote(
            grad_y.at[h, :, (y + j) % 4], grad_yrecv.at[k, j], gy_s.at[k, j], gy_r.at[k, j],
            y_peer(j),
        )

    for k in (2, 1, 3, 0):
        h = (zh + k) % 4
        grad_c(h).wait_recv()
        s = grad[h, :, :, core].astype(F32) + grad_core[h].astype(F32)
        grad_y[h] = s.astype(BF16)
        for j in (2, 1, 3):
            grad_yc(k, j).start()
        if k in (1, 3):
            dens_add(2 if k == 1 else 1)

    def grad_zc(k, m):
        t = (zl + m) % 4
        o = (4 * k + t - zl + 16) % 16
        return remote(
            grad_z.at[(zh + k) % 4, t], grad_zrecv.at[o], gz_s.at[o], gz_r.at[o], z_peer(o)
        )

    for k in (2, 1, 3, 0):
        h = (zh + k) % 4
        s = grad_y[h, :, y].astype(F32)
        for j in (1, 3, 2):
            grad_yc(k, j).wait_recv()
            s += grad_yrecv[k, j].astype(F32)
        grad_z[h] = s.astype(BF16)
        for m in range(4):
            if k or m:
                grad_zc(k, m).start()
        if k == 2:
            dens_add(3)
            dens_add(0)

    dens_out[zh] = dens_sum[zh]
    for k in (1, 3, 2):
        dens_z(k).wait_recv()
        dens_out[(zh - k + 4) % 4] = dens_zrecv[k]

    def grad_zo(o):
        return remote(
            grad_z.at[0, 0], grad_zrecv.at[o], gz_s.at[o], gz_r.at[o], z_peer(o)
        )

    def add_z(o, s):
        grad_zo(o).wait_recv()
        return s + grad_zrecv[o].astype(F32)

    s = lax.fori_loop(1, 16, add_z, grad_z[zh, zl].astype(F32))
    grad_out[0] = s[:, :64].astype(BF16)
    grad_out[1] = s[:, 64:].astype(BF16)

    for o in (1, 2, 3, 4, 5, 6, 7, 9, 10, 11, 12, 13, 14, 15):
        amp_z(o).wait_send()
    for n in range(2):
        amp_half(n).wait_send()
        int_relay(n).wait_send()
        int_onward(n).wait_send()

    @pl.loop(1, 16)
    def _(o):
        grad_zo(o).wait_send()

    @pl.loop(0, 16)
    def _(o):
        for j in (1, 2, 3):
            amp_y(o, j).wait_send()
        amp_c(o).wait_send()

    for k in range(4):
        for j in (1, 2, 3):
            int_x(k, j).wait_send()
            grad_yc(k, j).wait_send()
            dens_x(k, j).wait_send()
        grad_c(k).wait_send()
    for k in (1, 3):
        int_z(k).wait_send()
    for k in (1, 2, 3):
        dens_z(k).wait_send()


def local(i_list, pairs, vir_offsets, occ_energy, vir_energy, amplitudes, integrals):
    hbm = pl.BlockSpec(memory_space=pltpu.HBM)
    vmem = pl.BlockSpec(memory_space=pltpu.VMEM)
    dma = pltpu.SemaphoreType.DMA
    dens, grad = pl.pallas_call(
        kernel,
        out_shape=(
            jax.ShapeDtypeStruct((4, 64, 128), BF16),
            jax.ShapeDtypeStruct((2, 32, 64), BF16),
        ),
        in_specs=[hbm] * 8,
        out_specs=(vmem, vmem),
        scratch_shapes=[
            pltpu.SMEM((2,), jnp.int32), pltpu.SMEM((2, 2), jnp.int32),
            pltpu.SMEM((2,), jnp.int32), pltpu.SMEM((128,), F32), pltpu.SMEM((1024,), F32),
            pltpu.VMEM((8, 128), F32), pltpu.VMEM((2, 32, 64), BF16),
            pltpu.VMEM((2, 64, 2, 128), BF16), pltpu.VMEM((32, 128), BF16),
            pltpu.VMEM((4, 64, 128), BF16), dma((8,)),
            pltpu.VMEM((2, 32, 128), BF16), dma((2,)), dma((2,)),
            pltpu.VMEM((4, 4, 4, 2, 32, 128), BF16),
            pltpu.VMEM((16, 64, 128), BF16),
            pltpu.VMEM((4, 128, 128), BF16),
            pltpu.VMEM((4, 4, 4, 2, 32, 128), BF16),
            pltpu.VMEM((4, 4, 4, 32, 128), BF16),
            pltpu.VMEM((4, 4, 4, 32, 128), BF16),
            pltpu.VMEM((4, 4, 4, 32, 128), BF16),
            pltpu.VMEM((4, 4, 32, 128), BF16),
            pltpu.VMEM((16, 32, 128), BF16),
            pltpu.VMEM((4, 4, 64, 128), BF16),
            pltpu.VMEM((4, 4, 64, 128), BF16),
            pltpu.VMEM((4, 64, 128), BF16),
            pltpu.VMEM((4, 64, 128), BF16),
            dma((16,)), dma((16,)), dma((16, 4)), dma((16, 4)), dma((16,)), dma((16,)),
            dma((4,)), dma((4,)), dma((4, 4)), dma((4, 4)),
            dma((4, 4)), dma((4, 4)), dma((4,)), dma((4,)),
            dma((4,)), dma((4,)), dma((4, 4)), dma((4, 4)), dma((16,)), dma((16,)),
        ],
        compiler_params=pltpu.CompilerParams(collective_id=0, has_side_effects=True, vmem_limit_bytes=24 << 20),
    )(
        *(
            pltpu.with_memory_space_constraint(v, pltpu.HBM)
            for v in (
                i_list, pairs, vir_offsets, occ_energy, vir_energy, vir_energy.reshape(8, 128),
                amplitudes.transpose(0, 2, 1), integrals,
            )
        )
    )
    density = dens.reshape(2, 2, 64, 128).transpose(0, 2, 1, 3)
    return density, grad.transpose(0, 2, 1)


def solution(mesh):
    return jax.shard_map(
        local,
        mesh=mesh,
        in_specs=(P(), P(), P(), P(), P(), P(None, "row", "col"), P(None, "row", "col", None)),
        out_specs=(P(None, "row", "col", None), P(None, "row", "col")),
        check_vma=False,
    )
```
